32 devices in a mesh: band: 2 (over x), col: 16 (over z, y, core).
Axes of the slice: x: 2, y: 2, z: 4, core: 2. Of those that a mesh axis runs over, the one named last changes fastest.
Arguments:
- fields: bfloat16 [4, 80, 16, 2048], P(None, None, 'band', 'col'), may hold values from -6 to 6
- inverse: bfloat16 [4, 80, 80], replicated, may hold values from -1 to 2
- block_costs: int32 [16, 16], P('col', 'band'), may hold values from 1 to 8, as said below
- row_length: int32 [16], P('band'), may hold values from 1025 to 2048
Outputs:
- spectra: float32 [320, 16, 2, 512], P('col', None, None, 'band')
The draws below stay inside these ranges and needn't reach their ends.
Inputs may be any that keep to these rules, and one draw needn't show every extreme that they name: `block_costs`: at least one block takes 8 substeps and at least one takes 1.
All inputs are finite; a program needn't handle non-finite values.
Results may differ from the reference program's by a relative error of at most 0.0042.
Values may be sent and summed in bfloat16 or wider, within the bound.
A program may use at most 64 MiB of HBM per device.

```python
import math
import jax
import jax.numpy as jnp
from jax import lax

FIELDS = 4
LEV = 80
BLOCK = 128
CMAX = 8
ROWS = 16
NLON = 2048
WAVES = 512
N_COL = 16


def draw_inverse(key, part):
    key_diag, key_off = jax.random.split(jax.random.fold_in(key, 11))
    diagonal_part = 0.5 + 0.4 * jax.random.uniform(key_diag, (FIELDS, LEV), jnp.float32)
    off_part = jnp.clip(jax.random.normal(key_off, (FIELDS, LEV, LEV), jnp.float32), -1.7, 1.7) * 0.35
    off_part = off_part / jnp.sqrt(jnp.float32(LEV))
    identity = jnp.eye(LEV, dtype=jnp.float32)
    return (off_part + diagonal_part[:, :, None] * identity[None, :, :]).astype(jnp.bfloat16)


def draw_block_costs(key, part):
    key_heavy, key_cost = jax.random.split(jax.random.fold_in(key, 23))
    heavy_mask = jax.random.randint(key_heavy, (N_COL, 1), 0, 4) == 0
    top_cost = jnp.where(heavy_mask, CMAX, 1).astype(jnp.int32)
    costs_drawn = 1 + jax.random.randint(key_cost, (N_COL, ROWS), 0, top_cost)
    costs_drawn = costs_drawn.at[0, 0].set(CMAX).at[0, 1].set(1)
    return costs_drawn.astype(jnp.int32)


def set_ends(drawn, own_key, low, top_value):
    place = [jax.random.randint(jax.random.fold_in(own_key, axis), (), 0, length) for axis, length in enumerate(drawn.shape)]
    main_axis = drawn.shape.index(max(drawn.shape))
    next_to = place[:main_axis] + [(place[main_axis] + 1) % drawn.shape[main_axis]] + place[main_axis + 1:]
    return drawn.at[tuple(place)].set(low).at[tuple(next_to)].set(top_value)


def block_scale(stream_key, extent, cuts, smallest, largest):
    loudness, own = 1.0, jax.random.fold_in(stream_key, 6)
    for axis_at, shards_of in cuts:
        steps = jnp.exp(jax.random.uniform(jax.random.fold_in(own, axis_at), (shards_of,), jnp.float32, smallest / len(cuts), largest / len(cuts)))
        loudness = loudness * jnp.repeat(steps, extent[axis_at] // shards_of).reshape([-1 if axis == axis_at else 1 for axis in range(len(extent))])
    return loudness


def bell_draw(own_key, shape, width, limit, cuts=(), kind=jnp.bfloat16):
    drawn = width * jax.random.normal(own_key, shape, jnp.float32)
    if cuts:
        drawn = drawn * block_scale(own_key, shape, cuts, -0.22, 0.18)
    return jnp.clip(drawn, -limit, limit).astype(kind)


def setup_inputs(seed: int = 0) -> dict:
    key_list = jax.random.split(jax.random.key(seed), 5)
    return {
        "fields": bell_draw(key_list[0], (FIELDS, LEV, ROWS, NLON), 1.0, 6.0, ((2, 2), (3, 16))),
        "inverse": draw_inverse(jax.random.fold_in(key_list[4], 71), 0),
        "block_costs": draw_block_costs(jax.random.fold_in(key_list[4], 71), 0),
        "row_length": set_ends(jax.random.randint(key_list[3], (ROWS,), NLON // 2 + 1, NLON + 1), jax.random.fold_in(key_list[3], 1), NLON // 2 + 1, NLON).astype(jnp.int32),
    }


def reference(fields, inverse, block_costs, row_length):
    inverse_f32 = inverse.astype(jnp.float32)

    def row_spectrum(operands):
        field_row, cost_row, length_row = operands
        initial = field_row.reshape(FIELDS, LEV, N_COL, BLOCK)
        relaxed = initial
        for sweep_index in range(CMAX):
            applied = jnp.einsum('fkl,flcb->fkcb', inverse_f32, relaxed.astype(jnp.float32), precision=lax.Precision.HIGHEST).astype(jnp.bfloat16)
            relaxed = jnp.where((sweep_index < cost_row)[None, None, :, None], applied, relaxed)
        tendency = (relaxed.astype(jnp.float32) - initial.astype(jnp.float32)).astype(jnp.bfloat16)
        tendency = lax.optimization_barrier(tendency)
        updated = (initial.astype(jnp.float32) + tendency.astype(jnp.float32)).astype(jnp.bfloat16)
        updated = updated.reshape(FIELDS * LEV, NLON)
        longitude = jnp.arange(NLON, dtype=jnp.int32)
        masked = jnp.where(longitude[None, :] < length_row, updated, jnp.zeros_like(updated))
        spectrum = jnp.fft.rfft(masked.astype(jnp.float32), axis=-1)[:, :WAVES]
        scale_factor = 1.0 / math.sqrt(NLON)
        parts = jnp.stack([jnp.real(spectrum), jnp.imag(spectrum)], axis=1).astype(jnp.float32)
        return parts * scale_factor
    per_row = lax.map(row_spectrum, (jnp.moveaxis(fields, 2, 0), block_costs.T, row_length))
    return jnp.transpose(per_row, (1, 0, 2, 3))
```

```python
import functools
import math

import jax
import jax.numpy as jnp
import numpy as np
from jax import lax
from jax.experimental import pallas as pl
from jax.experimental.pallas import tpu as pltpu
from jax.sharding import PartitionSpec as P

sweep_total = 8
field_span = 1
table_limit = 4 * 1024 * 1024
spectral_vmem = 40 * 1024 * 1024
deliver_vmem = 8 * 1024 * 1024
MESH = pl.DeviceIdType.MESH


def spectral_kernel(
    col_total, band_total, scale, chunks,
    cost_ref, length_ref, fields_ref, inverse_ref, base_ref, phase_ref, out_ref,
    cost_buf, length_buf, inverse_buf, phase_buf,
    fields_buf, turn_in, turn_out, state_ref, blocks, landed, total, outgoing, incoming, base_buf, table_buf,
    field_sem, small_sem, base_sem, send_sem, recv_sem, band_send, band_recv,
):
    me, band = lax.axis_index("col"), lax.axis_index("band")
    field_total, level_total, row_total, width = fields_buf.shape
    own_levels = landed.shape[1]
    piece_width = total.shape[2]
    span = turn_in.shape[0]
    stages = field_total // span
    group = col_total // field_total
    place, inside = me // group, me % group
    toward = 1 - 2 * (place // (field_total // 2))
    middle = ((place + 1) // 2) % 2
    keep_table = table_buf.shape[0] == col_total * width

    barrier = pltpu.get_barrier_semaphore()

    def greet(t, carry):
        pl.semaphore_signal(
            barrier, inc=1, device_id={"col": (me + t) % col_total}, device_id_type=MESH
        )
        return carry

    lax.fori_loop(1, col_total, greet, 0)
    for j in range(1, band_total):
        pl.semaphore_signal(
            barrier, inc=1, device_id={"band": (band + j) % band_total}, device_id_type=MESH
        )

    def field_of(i):
        late = i // (field_total // 2)
        offset = (1 - late) * (field_total // 2 + i) + late * (field_total - 1 - i)
        return (place + field_total + toward * offset) % field_total

    def field_copy(i):
        return pltpu.make_async_copy(fields_ref.at[field_of(i)], fields_buf.at[i], field_sem.at[i])

    small = [
        pltpu.make_async_copy(source, target, small_sem.at[n])
        for n, (source, target) in enumerate(
            (
                (cost_ref, cost_buf), (length_ref, length_buf),
                (inverse_ref, inverse_buf), (phase_ref, phase_buf),
            )
        )
    ]
    field_copy(0).start()
    for copy in small[:3]:
        copy.start()
    for i in range(1, field_total):
        field_copy(i).start()
    base_copy = pltpu.make_async_copy(base_ref, base_buf, base_sem)
    small[3].start()
    base_copy.start()

    small[0].wait()
    small[1].wait()
    costs = jnp.concatenate(
        [jnp.full((1, width), cost_buf[0, r], jnp.int32) for r in range(row_total)], axis=1
    )
    longitude = me * width + lax.broadcasted_iota(jnp.int32, (1, width), 1)
    keep = jnp.concatenate(
        [(longitude < length_buf[r]).astype(jnp.int32) for r in range(row_total)], axis=0
    )[None] > 0
    small[2].wait()

    def relax(stage):
        for k in range(span):
            field_copy(span * stage + k).wait()
            turn_in[k] = (
                fields_buf[span * stage + k].astype(jnp.float32).reshape(level_total * row_total, width)
            )
        for k in range(span):
            for r in range(row_total):
                piece = turn_in[k, pl.ds(r, level_total, stride=row_total), :]
                state_ref[k, :, r * width : (r + 1) * width] = piece.astype(jnp.bfloat16)

        def sweep(s, carry):
            active = costs > s
            for k in range(span):
                before = state_ref[k]
                applied = jnp.dot(
                    inverse_buf[field_of(span * stage + k)], before, preferred_element_type=jnp.float32
                )
                state_ref[k] = jnp.where(
                    active, applied, before.astype(jnp.float32)
                ).astype(jnp.bfloat16)
            return carry

        lax.fori_loop(0, sweep_total, sweep, 0, unroll=True)
        for k in range(span):
            for r in range(row_total):
                turn_out[k, pl.ds(r, level_total, stride=row_total), :] = state_ref[
                    k, :, r * width : (r + 1) * width
                ].astype(jnp.float32)
        for k in range(span):
            f = field_of(span * stage + k)
            for q in range(group):
                rows = slice(q * own_levels * row_total, (q + 1) * own_levels * row_total)
                shape = (own_levels, row_total, width)
                initial = turn_in[k, rows, :].reshape(shape)
                tendency = (turn_out[k, rows, :].reshape(shape) - initial).astype(jnp.bfloat16)
                updated = initial + tendency.astype(jnp.float32)
                blocks[f * group + q] = jnp.where(keep, updated, 0.0).astype(jnp.bfloat16)

    def block_copy(chunk, peer, source):
        start, size = chunks[chunk]
        return pltpu.make_async_remote_copy(
            src_ref=blocks.at[peer, pl.ds(start, size)],
            dst_ref=landed.at[source, pl.ds(start, size)],
            send_sem=send_sem.at[chunk, peer],
            recv_sem=recv_sem.at[chunk, source],
            device_id={"col": peer},
            device_id_type=MESH,
        )

    def send_field(chunk, i, first):
        for j in range(first, group):
            peer = field_of(i) * group + (inside + j) % group
            block_copy(chunk, peer, me).start()

    def send_stage(stage, last):
        for k in range(span):
            send_field(0, span * stage + k, 1 if last and k == span - 1 else 0)

    def relax_and_send(stage, carry):
        relax(stage)
        send_stage(stage, False)
        return carry

    relax(0)
    pl.semaphore_wait(barrier, col_total - 1 + band_total - 1)
    send_stage(0, False)
    lax.fori_loop(1, stages - 1, relax_and_send, 0)
    relax(stages - 1)
    send_stage(stages - 1, True)

    for chunk in range(1, len(chunks)):
        def send_later(i, carry, chunk=chunk):
            send_field(chunk, i, 0)
            return carry

        lax.fori_loop(0, field_total - 1, send_later, 0)
        send_field(chunk, field_total - 1, 1)
    landed[me] = blocks[me]
    small[3].wait()
    base_copy.wait()

    def rows_of(source, chunk):
        start, size = chunks[chunk]
        values = landed[source, start : start + size].astype(jnp.float32)
        return values.reshape(size * row_total, width).astype(jnp.bfloat16)

    def accumulate(chunk, first, fresh):
        start, size = chunks[chunk]
        held = slice(start * row_total, (start + size) * row_total)
        rows = jnp.concatenate([rows_of(first, chunk), rows_of(first + 1, chunk)], axis=1)
        place_held = pl.ds(pl.multiple_of(first * width, width), 2 * width)
        for j in range(band_total):
            lanes = slice(j * piece_width, (j + 1) * piece_width)
            if keep_table and chunk > 0:
                table = table_buf[place_held, lanes]
            else:
                table = jnp.concatenate(
                    [
                        (
                            base_buf[0, :, lanes] * phase_buf[first + k, 0:1, lanes]
                            + base_buf[1, :, lanes] * phase_buf[first + k, 1:2, lanes]
                        ).astype(jnp.bfloat16)
                        for k in range(2)
                    ],
                    axis=0,
                )
                if keep_table:
                    table_buf[place_held, lanes] = table
            value = jnp.dot(rows, table, preferred_element_type=jnp.float32)
            total[j, held] = value if fresh else total[j, held] + value

    def band_copy(chunk, j, to_peer):
        start, size = chunks[chunk]
        held = pl.ds(start * row_total, size * row_total)
        peer = (band + j) % band_total
        origin = band if to_peer else peer
        return pltpu.make_async_remote_copy(
            src_ref=outgoing.at[peer, held],
            dst_ref=incoming.at[origin, held],
            send_sem=band_send.at[chunk, peer],
            recv_sem=band_recv.at[chunk, origin],
            device_id={"band": peer},
            device_id_type=MESH,
        )

    pairs = group // 2

    def first_of(t):
        g = t // pairs
        moved = ((g + field_total - 1) // field_total) * (g % (field_total - 1) + 1)
        offset = (1 - middle) * g + middle * moved
        source_place = (place + field_total + toward * offset) % field_total
        return source_place * group + 2 * ((inside // 2 + t % pairs) % pairs)

    mate = me + 1 - 2 * (me % 2)
    for chunk, (start, size) in enumerate(chunks):
        held = slice(start * row_total, (start + size) * row_total)
        block_copy(chunk, mate, mate).wait_recv()
        accumulate(chunk, first_of(0), True)

        def receive(t, carry, chunk=chunk):
            first = first_of(t)
            block_copy(chunk, first, first).wait_recv()
            block_copy(chunk, first + 1, first + 1).wait_recv()
            accumulate(chunk, first, False)
            return carry

        lax.fori_loop(1, col_total // 2, receive, 0)
        for j in range(1, band_total):
            peer = (band + j) % band_total
            outgoing[peer, held] = (total[peer, held] * scale).astype(jnp.bfloat16)
        for j in range(1, band_total):
            band_copy(chunk, j, True).start()

    def put(origin, start, size, values):
        pieces = piece_width // 128
        for level in range(size):
            rows = values[level * row_total : (level + 1) * row_total]
            for k in range(pieces):
                out_ref[start + level, origin, pl.ds(k, row_total, stride=pieces), :] = rows[
                    :, k * 128 : (k + 1) * 128
                ]

    for start, size in chunks:
        held = slice(start * row_total, (start + size) * row_total)
        put(band, start, size, total[band, held] * scale)

    def drain(t, carry):
        peer = (me + t) % col_total
        for chunk in range(len(chunks)):
            block_copy(chunk, peer, me).wait_send()
        return carry

    lax.fori_loop(1, col_total, drain, 0)
    for chunk, (start, size) in enumerate(chunks):
        held = slice(start * row_total, (start + size) * row_total)
        for j in range(1, band_total):
            peer = (band + j) % band_total
            band_copy(chunk, j, False).wait_recv()
            put(peer, start, size, incoming[peer, held].astype(jnp.float32))
    for chunk in range(len(chunks)):
        for j in range(1, band_total):
            band_copy(chunk, j, True).wait_send()


def deliver_kernel(size, held, out_ref, out_sem):
    parts = [pl.ds(p * size, size) for p in range(held.shape[0] // size)]
    writes = [
        pltpu.make_async_copy(held.at[part], out_ref.at[part], out_sem.at[p])
        for p, part in enumerate(parts)
    ]
    for write in writes:
        write.start()
    for write in writes:
        write.wait()


def level_chunks(own_levels):
    last = max(1, own_levels // 5)
    head = (own_levels - last + 1) // 2
    sizes = [n for n in (head, own_levels - last - head, last) if n > 0]
    return tuple((sum(sizes[:i]), n) for i, n in enumerate(sizes))


def tables(width, col_total, band_total):
    length = width * col_total
    waves = np.arange(length // 4, dtype=np.int64).reshape(-1, 1, 128)
    shape = (waves.shape[0], 2, 128)
    wave_of = np.broadcast_to(waves, shape).reshape(-1)
    imaginary = np.broadcast_to(np.arange(2).reshape(1, 2, 1), shape).reshape(-1)
    angle = 2.0 * np.pi * ((np.arange(width)[:, None] * wave_of[None, :]) % length) / length
    cosine, sine = np.cos(angle), np.sin(angle)
    plain = np.where(imaginary[None, :] == 1, -sine, cosine)
    crossed = np.where(imaginary[None, :] == 1, -cosine, -sine)
    base = np.stack([plain, crossed])
    turn = 2.0 * np.pi * ((np.arange(col_total)[:, None] * wave_of[None, :]) % col_total) / col_total
    phase = np.stack([np.cos(turn), np.sin(turn)], axis=1)
    return base.astype(np.float32), phase.astype(np.float32)


def shards(fields, inverse, block_costs, row_length):
    field_total, level_total, row_total, width = fields.shape
    col_total, band_total = lax.axis_size("col"), lax.axis_size("band")
    own_levels = field_total * level_total // col_total
    vmem = pl.BlockSpec(memory_space=pltpu.VMEM)
    hbm = pl.BlockSpec(memory_space=pl.ANY)
    base, phase = tables(width, col_total, band_total)
    own_rows, piece_width = own_levels * row_total, base.shape[2] // band_total
    waves = piece_width // 2
    chunks = level_chunks(own_levels)
    table_shape = (col_total * width, base.shape[2])
    if table_shape[0] * table_shape[1] > table_limit:
        table_shape = (16, 128)
    shape = (own_levels, band_total, row_total * piece_width // 128, 128)
    spectra = pl.pallas_call(
        functools.partial(
            spectral_kernel, col_total, band_total, 1.0 / math.sqrt(width * col_total), chunks
        ),
        name="spectral",
        out_shape=pltpu.VMEM(shape, jnp.float32),
        in_specs=[hbm] * 6,
        out_specs=vmem,
        scratch_shapes=[
            pltpu.SMEM(block_costs.shape, jnp.int32),
            pltpu.SMEM(row_length.shape, jnp.int32),
            pltpu.VMEM(inverse.shape, jnp.bfloat16),
            pltpu.VMEM(phase.shape, jnp.float32),
            pltpu.VMEM(fields.shape, jnp.bfloat16),
            pltpu.VMEM((field_span, level_total * row_total, width), jnp.float32),
            pltpu.VMEM((field_span, level_total * row_total, width), jnp.float32),
            pltpu.VMEM((field_span, level_total, row_total * width), jnp.bfloat16),
            pltpu.VMEM((col_total, own_levels, row_total, width), jnp.bfloat16),
            pltpu.VMEM((col_total, own_levels, row_total, width), jnp.bfloat16),
            pltpu.VMEM((band_total, own_rows, piece_width), jnp.float32),
            pltpu.VMEM((band_total, own_rows, piece_width), jnp.bfloat16),
            pltpu.VMEM((band_total, own_rows, piece_width), jnp.bfloat16),
            pltpu.VMEM(base.shape, jnp.float32),
            pltpu.VMEM(table_shape, jnp.bfloat16),
            pltpu.SemaphoreType.DMA((field_total,)),
            pltpu.SemaphoreType.DMA((4,)),
            pltpu.SemaphoreType.DMA,
            pltpu.SemaphoreType.DMA((len(chunks), col_total)),
            pltpu.SemaphoreType.DMA((len(chunks), col_total)),
            pltpu.SemaphoreType.DMA((len(chunks), band_total)),
            pltpu.SemaphoreType.DMA((len(chunks), band_total)),
        ],
        compiler_params=pltpu.CompilerParams(
            collective_id=0, has_side_effects=True, vmem_limit_bytes=spectral_vmem
        ),
    )(
        *(
            pltpu.with_memory_space_constraint(value, pltpu.HBM)
            for value in (block_costs, row_length, fields, inverse, jnp.asarray(base), jnp.asarray(phase))
        )
    )
    pieces = next(p for p in (5, 4, 2, 1) if own_levels % p == 0)
    spectra = pl.pallas_call(
        functools.partial(deliver_kernel, own_levels // pieces),
        name="deliver",
        out_shape=jax.ShapeDtypeStruct(spectra.shape, spectra.dtype),
        in_specs=[vmem],
        out_specs=hbm,
        scratch_shapes=[pltpu.SemaphoreType.DMA((pieces,))],
        compiler_params=pltpu.CompilerParams(vmem_limit_bytes=deliver_vmem),
    )(spectra)
    split = spectra.reshape(own_levels, band_total * row_total, waves // 128, 2, 128)
    return split.transpose(0, 1, 3, 2, 4).reshape(own_levels, band_total * row_total, 2, waves)


def solution(mesh):
    return jax.shard_map(
        shards,
        mesh=mesh,
        in_specs=(P(None, None, "band", "col"), P(), P("col", "band"), P("band")),
        out_specs=P("col", None, None, "band"),
        check_vma=False,
    )
```

```python
import functools
import math

import jax
import jax.numpy as jnp
import numpy as np
from jax import lax
from jax.experimental import pallas as pl
from jax.experimental.pallas import tpu as pltpu
from jax.sharding import PartitionSpec as P

sweep_total = 8
field_span = 2
table_limit = 4 * 1024 * 1024
spectral_vmem = 40 * 1024 * 1024
deliver_vmem = 8 * 1024 * 1024
MESH = pl.DeviceIdType.MESH


def spectral_kernel(
    col_total, band_total, scale, chunks,
    cost_ref, length_ref, fields_ref, inverse_ref, base_ref, phase_ref, out_ref,
    cost_buf, length_buf, inverse_buf, phase_buf,
    fields_buf, turn_in, turn_out, state_ref, blocks, landed, total, outgoing, incoming, base_buf, table_buf,
    field_sem, small_sem, base_sem, send_sem, recv_sem, band_send, band_recv,
):
    me, band = lax.axis_index("col"), lax.axis_index("band")
    field_total, level_total, row_total, width = fields_buf.shape
    own_levels = landed.shape[1]
    piece_width = total.shape[2]
    span = turn_in.shape[0]
    stages = field_total // span
    group = col_total // field_total
    place, inside = me // group, me % group
    toward = 1 - 2 * (place // (field_total // 2))
    middle = ((place + 1) // 2) % 2
    batch = min(group, 4)
    keep_table = table_buf.shape[0] == col_total * width

    barrier = pltpu.get_barrier_semaphore()

    def greet(t, carry):
        pl.semaphore_signal(
            barrier, inc=1, device_id={"col": (me + t) % col_total}, device_id_type=MESH
        )
        return carry

    lax.fori_loop(1, col_total, greet, 0)
    for j in range(1, band_total):
        pl.semaphore_signal(
            barrier, inc=1, device_id={"band": (band + j) % band_total}, device_id_type=MESH
        )

    def field_of(i):
        late = i // (field_total // 2)
        offset = (1 - late) * (field_total // 2 + i) + late * (field_total - 1 - i)
        return (place + field_total + toward * offset) % field_total

    def field_copy(i):
        return pltpu.make_async_copy(fields_ref.at[field_of(i)], fields_buf.at[i], field_sem.at[i])

    small = [
        pltpu.make_async_copy(source, target, small_sem.at[n])
        for n, (source, target) in enumerate(
            (
                (cost_ref, cost_buf), (length_ref, length_buf),
                (inverse_ref, inverse_buf), (phase_ref, phase_buf),
            )
        )
    ]
    field_copy(0).start()
    for copy in small[:3]:
        copy.start()
    for i in range(1, field_total):
        field_copy(i).start()
    base_copy = pltpu.make_async_copy(base_ref, base_buf, base_sem)
    small[3].start()
    base_copy.start()

    small[0].wait()
    small[1].wait()
    costs = jnp.concatenate(
        [jnp.full((1, width), cost_buf[0, r], jnp.int32) for r in range(row_total)], axis=1
    )
    longitude = me * width + lax.broadcasted_iota(jnp.int32, (1, width), 1)
    keep = jnp.concatenate(
        [(longitude < length_buf[r]).astype(jnp.int32) for r in range(row_total)], axis=0
    )[None] > 0
    small[2].wait()

    def relax(stage):
        for k in range(span):
            field_copy(span * stage + k).wait()
            turn_in[k] = (
                fields_buf[span * stage + k].astype(jnp.float32).reshape(level_total * row_total, width)
            )
        for k in range(span):
            for r in range(row_total):
                piece = turn_in[k, pl.ds(r, level_total, stride=row_total), :]
                state_ref[k, :, r * width : (r + 1) * width] = piece.astype(jnp.bfloat16)

        def sweep(s, carry):
            active = costs > s
            for k in range(span):
                before = state_ref[k]
                applied = jnp.dot(
                    inverse_buf[field_of(span * stage + k)], before, preferred_element_type=jnp.float32
                )
                state_ref[k] = jnp.where(
                    active, applied, before.astype(jnp.float32)
                ).astype(jnp.bfloat16)
            return carry

        lax.fori_loop(0, sweep_total, sweep, 0, unroll=True)
        for k in range(span):
            for r in range(row_total):
                turn_out[k, pl.ds(r, level_total, stride=row_total), :] = state_ref[
                    k, :, r * width : (r + 1) * width
                ].astype(jnp.float32)
        for k in range(span):
            f = field_of(span * stage + k)
            for q in range(group):
                rows = slice(q * own_levels * row_total, (q + 1) * own_levels * row_total)
                shape = (own_levels, row_total, width)
                initial = turn_in[k, rows, :].reshape(shape)
                tendency = (turn_out[k, rows, :].reshape(shape) - initial).astype(jnp.bfloat16)
                updated = initial + tendency.astype(jnp.float32)
                blocks[f * group + q] = jnp.where(keep, updated, 0.0).astype(jnp.bfloat16)

    def block_copy(chunk, peer, source):
        start, size = chunks[chunk]
        return pltpu.make_async_remote_copy(
            src_ref=blocks.at[peer, pl.ds(start, size)],
            dst_ref=landed.at[source, pl.ds(start, size)],
            send_sem=send_sem,
            recv_sem=recv_sem.at[chunk, source // batch],
            device_id={"col": peer},
            device_id_type=MESH,
        )

    def send_field(chunk_set, i, first):
        for chunk in chunk_set:
            for j in range(first, group):
                peer = field_of(i) * group + (inside + j) % group
                block_copy(chunk, peer, me).start()

    def send_stage(stage, last):
        for k in range(span):
            send_field((0,), span * stage + k, 1 if last and k == span - 1 else 0)

    def relax_and_send(stage, carry):
        relax(stage)
        send_stage(stage, False)
        return carry

    relax(0)
    pl.semaphore_wait(barrier, col_total - 1 + band_total - 1)
    send_stage(0, False)
    lax.fori_loop(1, stages - 1, relax_and_send, 0)
    relax(stages - 1)
    send_stage(stages - 1, True)
    later = range(1, len(chunks))

    def send_later(i, carry):
        send_field(later, i, 0)
        return carry

    lax.fori_loop(0, field_total - 1, send_later, 0)
    send_field(later, field_total - 1, 1)
    landed[me] = blocks[me]
    small[3].wait()
    base_copy.wait()

    def rows_of(source, chunk):
        start, size = chunks[chunk]
        values = landed[source, start : start + size].astype(jnp.float32)
        return values.reshape(size * row_total, width).astype(jnp.bfloat16)

    def accumulate(chunk, first, fresh):
        start, size = chunks[chunk]
        held = slice(start * row_total, (start + size) * row_total)
        rows = jnp.concatenate([rows_of(first + k, chunk) for k in range(batch)], axis=1)
        for j in range(band_total):
            lanes = slice(j * piece_width, (j + 1) * piece_width)
            kept = pl.ds(pl.multiple_of(first * width, batch * width), batch * width)
            if keep_table and chunk > 0:
                table = table_buf[kept, lanes]
            else:
                table = jnp.concatenate(
                    [
                        (
                            base_buf[0, :, lanes] * phase_buf[first + k, 0:1, lanes]
                            + base_buf[1, :, lanes] * phase_buf[first + k, 1:2, lanes]
                        ).astype(jnp.bfloat16)
                        for k in range(batch)
                    ],
                    axis=0,
                )
                if keep_table:
                    table_buf[kept, lanes] = table
            value = jnp.dot(rows, table, preferred_element_type=jnp.float32)
            total[j, held] = value if fresh else total[j, held] + value

    def band_copy(chunk, j, to_peer):
        start, size = chunks[chunk]
        held = pl.ds(start * row_total, size * row_total)
        peer = (band + j) % band_total
        origin = band if to_peer else peer
        return pltpu.make_async_remote_copy(
            src_ref=outgoing.at[peer, held],
            dst_ref=incoming.at[origin, held],
            send_sem=band_send.at[chunk, peer],
            recv_sem=band_recv.at[chunk, origin],
            device_id={"band": peer},
            device_id_type=MESH,
        )

    batches = group // batch

    def first_of(g, t):
        moved = ((g + field_total - 1) // field_total) * (g % (field_total - 1) + 1)
        offset = (1 - middle) * g + middle * moved
        source_place = (place + field_total + toward * offset) % field_total
        return source_place * group + batch * ((inside // batch + t) % batches)

    def await_blocks(chunk, source, first, count):
        start, size = chunks[chunk]
        blocks_in = landed.at[pl.ds(first, count), pl.ds(start, size)]
        pltpu.make_async_copy(blocks_in, blocks_in, recv_sem.at[chunk, source // batch]).wait()

    def receive(chunk, g, t):
        first = first_of(g, t)
        await_blocks(chunk, first, first, batch)
        accumulate(chunk, first, False)

    def receive_group(chunk, g):
        if g == 0:
            await_blocks(chunk, me, 0, batch - 1)
            accumulate(chunk, first_of(0, 0), True)
        first_step = 1 if g == 0 else 0
        if batches - first_step == 1:
            receive(chunk, g, first_step)
        elif batches - first_step > 1:

            def body(t, carry):
                receive(chunk, g, t)
                return carry

            lax.fori_loop(first_step, batches, body, 0)

    def hand_over(chunk):
        start, size = chunks[chunk]
        held = slice(start * row_total, (start + size) * row_total)
        for j in range(1, band_total):
            peer = (band + j) % band_total
            outgoing[peer, held] = (total[peer, held] * scale).astype(jnp.bfloat16)
        for j in range(1, band_total):
            band_copy(chunk, j, True).start()

    order = [(0, g) for g in range(field_total)]
    order += [(chunk, g) for g in range(field_total // 2) for chunk in later]
    order += [(chunk, g) for chunk in later for g in range(field_total // 2, field_total)]
    for chunk, g in order:
        receive_group(chunk, g)
        if g == field_total - 1:
            hand_over(chunk)

    def put(origin, start, size, values):
        pieces = piece_width // 128
        for level in range(size):
            rows = values[level * row_total : (level + 1) * row_total]
            for k in range(pieces):
                out_ref[start + level, origin, pl.ds(k, row_total, stride=pieces), :] = rows[
                    :, k * 128 : (k + 1) * 128
                ]

    for start, size in chunks:
        held = slice(start * row_total, (start + size) * row_total)
        put(band, start, size, total[band, held] * scale)

    sent = blocks.at[pl.ds(0, col_total - 1)]
    pltpu.make_async_copy(sent, sent, send_sem).wait()
    for chunk, (start, size) in enumerate(chunks):
        held = slice(start * row_total, (start + size) * row_total)
        for j in range(1, band_total):
            peer = (band + j) % band_total
            band_copy(chunk, j, False).wait_recv()
            put(peer, start, size, incoming[peer, held].astype(jnp.float32))
    for chunk in range(len(chunks)):
        for j in range(1, band_total):
            band_copy(chunk, j, True).wait_send()


def deliver_kernel(size, held, out_ref, out_sem):
    parts = [pl.ds(p * size, size) for p in range(held.shape[0] // size)]
    writes = [
        pltpu.make_async_copy(held.at[part], out_ref.at[part], out_sem.at[p])
        for p, part in enumerate(parts)
    ]
    for write in writes:
        write.start()
    for write in writes:
        write.wait()


def level_chunks(own_levels):
    last = max(1, own_levels // 5)
    sizes = [own_levels - 2 * last, last, last]
    return tuple((sum(sizes[:i]), n) for i, n in enumerate(sizes) if n > 0)


def tables(width, col_total, band_total):
    length = width * col_total
    waves = np.arange(length // 4, dtype=np.int64).reshape(-1, 1, 128)
    shape = (waves.shape[0], 2, 128)
    wave_of = np.broadcast_to(waves, shape).reshape(-1)
    imaginary = np.broadcast_to(np.arange(2).reshape(1, 2, 1), shape).reshape(-1)
    angle = 2.0 * np.pi * ((np.arange(width)[:, None] * wave_of[None, :]) % length) / length
    cosine, sine = np.cos(angle), np.sin(angle)
    plain = np.where(imaginary[None, :] == 1, -sine, cosine)
    crossed = np.where(imaginary[None, :] == 1, -cosine, -sine)
    base = np.stack([plain, crossed])
    turn = 2.0 * np.pi * ((np.arange(col_total)[:, None] * wave_of[None, :]) % col_total) / col_total
    phase = np.stack([np.cos(turn), np.sin(turn)], axis=1)
    return base.astype(np.float32), phase.astype(np.float32)


def shards(fields, inverse, block_costs, row_length):
    field_total, level_total, row_total, width = fields.shape
    col_total, band_total = lax.axis_size("col"), lax.axis_size("band")
    own_levels = field_total * level_total // col_total
    vmem = pl.BlockSpec(memory_space=pltpu.VMEM)
    hbm = pl.BlockSpec(memory_space=pl.ANY)
    base, phase = tables(width, col_total, band_total)
    own_rows, piece_width = own_levels * row_total, base.shape[2] // band_total
    waves = piece_width // 2
    chunks = level_chunks(own_levels)
    table_shape = (col_total * width, base.shape[2])
    if table_shape[0] * table_shape[1] > table_limit:
        table_shape = (16, 128)
    shape = (own_levels, band_total, row_total * piece_width // 128, 128)
    spectra = pl.pallas_call(
        functools.partial(
            spectral_kernel, col_total, band_total, 1.0 / math.sqrt(width * col_total), chunks
        ),
        name="spectral",
        out_shape=pltpu.VMEM(shape, jnp.float32),
        in_specs=[hbm] * 6,
        out_specs=vmem,
        scratch_shapes=[
            pltpu.SMEM(block_costs.shape, jnp.int32),
            pltpu.SMEM(row_length.shape, jnp.int32),
            pltpu.VMEM(inverse.shape, jnp.bfloat16),
            pltpu.VMEM(phase.shape, jnp.float32),
            pltpu.VMEM(fields.shape, jnp.bfloat16),
            pltpu.VMEM((field_span, level_total * row_total, width), jnp.float32),
            pltpu.VMEM((field_span, level_total * row_total, width), jnp.float32),
            pltpu.VMEM((field_span, level_total, row_total * width), jnp.bfloat16),
            pltpu.VMEM((col_total, own_levels, row_total, width), jnp.bfloat16),
            pltpu.VMEM((col_total, own_levels, row_total, width), jnp.bfloat16),
            pltpu.VMEM((band_total, own_rows, piece_width), jnp.float32),
            pltpu.VMEM((band_total, own_rows, piece_width), jnp.bfloat16),
            pltpu.VMEM((band_total, own_rows, piece_width), jnp.bfloat16),
            pltpu.VMEM(base.shape, jnp.float32),
            pltpu.VMEM(table_shape, jnp.bfloat16),
            pltpu.SemaphoreType.DMA((field_total,)),
            pltpu.SemaphoreType.DMA((4,)),
            pltpu.SemaphoreType.DMA,
            pltpu.SemaphoreType.DMA,
            pltpu.SemaphoreType.DMA((len(chunks), col_total // min(col_total // field_total, 4))),
            pltpu.SemaphoreType.DMA((len(chunks), band_total)),
            pltpu.SemaphoreType.DMA((len(chunks), band_total)),
        ],
        compiler_params=pltpu.CompilerParams(
            collective_id=0, has_side_effects=True, vmem_limit_bytes=spectral_vmem
        ),
    )(
        *(
            pltpu.with_memory_space_constraint(value, pltpu.HBM)
            for value in (block_costs, row_length, fields, inverse, jnp.asarray(base), jnp.asarray(phase))
        )
    )
    pieces = next(p for p in (5, 4, 2, 1) if own_levels % p == 0)
    spectra = pl.pallas_call(
        functools.partial(deliver_kernel, own_levels // pieces),
        name="deliver",
        out_shape=jax.ShapeDtypeStruct(spectra.shape, spectra.dtype),
        in_specs=[vmem],
        out_specs=hbm,
        scratch_shapes=[pltpu.SemaphoreType.DMA((pieces,))],
        compiler_params=pltpu.CompilerParams(vmem_limit_bytes=deliver_vmem),
    )(spectra)
    split = spectra.reshape(own_levels, band_total * row_total, waves // 128, 2, 128)
    return split.transpose(0, 1, 3, 2, 4).reshape(own_levels, band_total * row_total, 2, waves)


def solution(mesh):
    return jax.shard_map(
        shards,
        mesh=mesh,
        in_specs=(P(None, None, "band", "col"), P(), P("col", "band"), P("band")),
        out_specs=P("col", None, None, "band"),
        check_vma=False,
    )
```

```python
import functools
import math

import jax
import jax.numpy as jnp
import numpy as np
from jax import lax
from jax.experimental import pallas as pl
from jax.experimental.pallas import tpu as pltpu
from jax.sharding import PartitionSpec as P

sweep_total = 8
field_span = 2
far_after = 2
near_after = 3
table_limit = 4 * 1024 * 1024
spectral_vmem = 40 * 1024 * 1024
deliver_vmem = 8 * 1024 * 1024
MESH = pl.DeviceIdType.MESH


def spectral_kernel(
    col_total, band_total, scale, chunks,
    cost_ref, length_ref, fields_ref, inverse_ref, base_ref, phase_ref, out_ref,
    cost_buf, length_buf, inverse_buf, phase_buf,
    fields_buf, turn_in, turn_out, state_ref, blocks, landed, total, outgoing, incoming, base_buf, table_buf,
    field_sem, small_sem, base_sem, send_sem, recv_sem, band_send, band_recv,
):
    me, band = lax.axis_index("col"), lax.axis_index("band")
    field_total, level_total, row_total, width = fields_buf.shape
    own_levels = landed.shape[1]
    piece_width = total.shape[2]
    span = turn_in.shape[0]
    stages = field_total // span
    group = col_total // field_total
    place, inside = me // group, me % group
    toward = 1 - 2 * (place // (field_total // 2))
    middle = ((place + 1) // 2) % 2
    batch = min(group, 4)
    keep_table = table_buf.shape[0] == col_total * width

    barrier = pltpu.get_barrier_semaphore()

    def greet(t, carry):
        pl.semaphore_signal(
            barrier, inc=1, device_id={"col": (me + t) % col_total}, device_id_type=MESH
        )
        return carry

    lax.fori_loop(1, col_total, greet, 0)
    for j in range(1, band_total):
        pl.semaphore_signal(
            barrier, inc=1, device_id={"band": (band + j) % band_total}, device_id_type=MESH
        )

    def field_of(i):
        late = i // (field_total // 2)
        offset = (1 - late) * (field_total // 2 + i) + late * (field_total - 1 - i)
        return (place + field_total + toward * offset) % field_total

    def field_copy(i):
        return pltpu.make_async_copy(fields_ref.at[field_of(i)], fields_buf.at[i], field_sem.at[i])

    small = [
        pltpu.make_async_copy(source, target, small_sem.at[n])
        for n, (source, target) in enumerate(
            (
                (cost_ref, cost_buf), (length_ref, length_buf),
                (inverse_ref, inverse_buf), (phase_ref, phase_buf),
            )
        )
    ]
    field_copy(0).start()
    for copy in small[:3]:
        copy.start()
    for i in range(1, field_total):
        field_copy(i).start()
    base_copy = pltpu.make_async_copy(base_ref, base_buf, base_sem)
    small[3].start()
    base_copy.start()

    small[0].wait()
    small[1].wait()
    costs = jnp.concatenate(
        [jnp.full((1, width), cost_buf[0, r], jnp.int32) for r in range(row_total)], axis=1
    )
    longitude = me * width + lax.broadcasted_iota(jnp.int32, (1, width), 1)
    keep = jnp.concatenate(
        [(longitude < length_buf[r]).astype(jnp.int32) for r in range(row_total)], axis=0
    )[None] > 0
    small[2].wait()

    def relax(stage):
        for k in range(span):
            field_copy(span * stage + k).wait()
            turn_in[k] = (
                fields_buf[span * stage + k].astype(jnp.float32).reshape(level_total * row_total, width)
            )
        for k in range(span):
            for r in range(row_total):
                piece = turn_in[k, pl.ds(r, level_total, stride=row_total), :]
                state_ref[k, :, r * width : (r + 1) * width] = piece.astype(jnp.bfloat16)

        def sweep(s, carry):
            active = costs > s
            for k in range(span):
                before = state_ref[k]
                applied = jnp.dot(
                    inverse_buf[field_of(span * stage + k)], before, preferred_element_type=jnp.float32
                )
                state_ref[k] = jnp.where(
                    active, applied, before.astype(jnp.float32)
                ).astype(jnp.bfloat16)
            return carry

        lax.fori_loop(0, sweep_total, sweep, 0, unroll=True)
        for k in range(span):
            for r in range(row_total):
                turn_out[k, pl.ds(r, level_total, stride=row_total), :] = state_ref[
                    k, :, r * width : (r + 1) * width
                ].astype(jnp.float32)
        for k in range(span):
            f = field_of(span * stage + k)
            for q in range(group):
                rows = slice(q * own_levels * row_total, (q + 1) * own_levels * row_total)
                shape = (own_levels, row_total, width)
                initial = turn_in[k, rows, :].reshape(shape)
                tendency = (turn_out[k, rows, :].reshape(shape) - initial).astype(jnp.bfloat16)
                updated = initial + tendency.astype(jnp.float32)
                blocks[f * group + q] = jnp.where(keep, updated, 0.0).astype(jnp.bfloat16)

    def block_copy(chunk, peer, source):
        start, size = chunks[chunk]
        return pltpu.make_async_remote_copy(
            src_ref=blocks.at[peer, pl.ds(start, size)],
            dst_ref=landed.at[source, pl.ds(start, size)],
            send_sem=send_sem,
            recv_sem=recv_sem.at[chunk, source // batch],
            device_id={"col": peer},
            device_id_type=MESH,
        )

    def send_field(chunk_set, i, first):
        for chunk in chunk_set:
            for j in range(first, group):
                peer = field_of(i) * group + (inside + j) % group
                block_copy(chunk, peer, me).start()

    def send_stage(stage, last):
        for k in range(span):
            send_field((0,), span * stage + k, 1 if last and k == span - 1 else 0)

    def relax_and_send(stage, carry):
        relax(stage)
        send_stage(stage, False)
        return carry

    relax(0)
    pl.semaphore_wait(barrier, col_total - 1 + band_total - 1)
    send_stage(0, False)
    lax.fori_loop(1, stages - 1, relax_and_send, 0)
    relax(stages - 1)
    send_stage(stages - 1, True)
    later = range(1, len(chunks))


    def send_later(i, carry):
        send_field(later, i, 0)
        return carry

    landed[me] = blocks[me]
    small[3].wait()
    base_copy.wait()

    def rows_of(source, chunk):
        start, size = chunks[chunk]
        values = landed[source, start : start + size].astype(jnp.float32)
        return values.reshape(size * row_total, width).astype(jnp.bfloat16)

    def accumulate(chunk, first, fresh):
        start, size = chunks[chunk]
        held = slice(start * row_total, (start + size) * row_total)
        rows = jnp.concatenate([rows_of(first + k, chunk) for k in range(batch)], axis=1)
        for j in range(band_total):
            lanes = slice(j * piece_width, (j + 1) * piece_width)
            kept = pl.ds(pl.multiple_of(first * width, batch * width), batch * width)
            if keep_table and chunk > 0:
                table = table_buf[kept, lanes]
            else:
                table = jnp.concatenate(
                    [
                        (
                            base_buf[0, :, lanes] * phase_buf[first + k, 0:1, lanes]
                            + base_buf[1, :, lanes] * phase_buf[first + k, 1:2, lanes]
                        ).astype(jnp.bfloat16)
                        for k in range(batch)
                    ],
                    axis=0,
                )
                if keep_table:
                    table_buf[kept, lanes] = table
            value = jnp.dot(rows, table, preferred_element_type=jnp.float32)
            total[j, held] = value if fresh else total[j, held] + value

    def band_copy(chunk, j, to_peer):
        start, size = chunks[chunk]
        held = pl.ds(start * row_total, size * row_total)
        peer = (band + j) % band_total
        origin = band if to_peer else peer
        return pltpu.make_async_remote_copy(
            src_ref=outgoing.at[peer, held],
            dst_ref=incoming.at[origin, held],
            send_sem=band_send.at[chunk, peer],
            recv_sem=band_recv.at[chunk, origin],
            device_id={"band": peer},
            device_id_type=MESH,
        )

    batches = group // batch

    def first_of(g, t):
        moved = ((g + field_total - 1) // field_total) * (g % (field_total - 1) + 1)
        offset = (1 - middle) * g + middle * moved
        source_place = (place + field_total + toward * offset) % field_total
        return source_place * group + batch * ((inside // batch + t) % batches)

    def await_blocks(chunk, source, first, count):
        start, size = chunks[chunk]
        blocks_in = landed.at[pl.ds(first, count), pl.ds(start, size)]
        pltpu.make_async_copy(blocks_in, blocks_in, recv_sem.at[chunk, source // batch]).wait()

    def receive(chunk, g, t):
        first = first_of(g, t)
        await_blocks(chunk, first, first, batch)
        accumulate(chunk, first, False)

    def receive_group(chunk, g):
        if g == 0:
            await_blocks(chunk, me, 0, batch - 1)
            accumulate(chunk, first_of(0, 0), True)
        first_step = 1 if g == 0 else 0
        if batches - first_step == 1:
            receive(chunk, g, first_step)
        elif batches - first_step > 1:

            def body(t, carry):
                receive(chunk, g, t)
                return carry

            lax.fori_loop(first_step, batches, body, 0)

    def hand_over(chunk):
        start, size = chunks[chunk]
        held = slice(start * row_total, (start + size) * row_total)
        for j in range(1, band_total):
            peer = (band + j) % band_total
            outgoing[peer, held] = (total[peer, held] * scale).astype(jnp.bfloat16)
        for j in range(1, band_total):
            band_copy(chunk, j, True).start()

    order = [(0, g) for g in range(field_total)]
    order += [(chunk, g) for g in range(field_total // 2) for chunk in later]
    order += [(chunk, g) for chunk in later for g in range(field_total // 2, field_total)]
    for chunk, g in order:
        receive_group(chunk, g)
        if (chunk, g) == (0, far_after):
            lax.fori_loop(0, field_total // 2, send_later, 0)
        if (chunk, g) == (0, near_after):
            lax.fori_loop(field_total // 2, field_total - 1, send_later, 0)
            send_field(later, field_total - 1, 1)
        if g == field_total - 1:
            hand_over(chunk)

    def put(origin, start, size, values):
        pieces = piece_width // 128
        for level in range(size):
            rows = values[level * row_total : (level + 1) * row_total]
            for k in range(pieces):
                out_ref[start + level, origin, pl.ds(k, row_total, stride=pieces), :] = rows[
                    :, k * 128 : (k + 1) * 128
                ]

    for start, size in chunks:
        held = slice(start * row_total, (start + size) * row_total)
        put(band, start, size, total[band, held] * scale)

    sent = blocks.at[pl.ds(0, col_total - 1)]
    pltpu.make_async_copy(sent, sent, send_sem).wait()
    for chunk, (start, size) in enumerate(chunks):
        held = slice(start * row_total, (start + size) * row_total)
        for j in range(1, band_total):
            peer = (band + j) % band_total
            band_copy(chunk, j, False).wait_recv()
            put(peer, start, size, incoming[peer, held].astype(jnp.float32))
    for chunk in range(len(chunks)):
        for j in range(1, band_total):
            band_copy(chunk, j, True).wait_send()


def deliver_kernel(size, held, out_ref, out_sem):
    parts = [pl.ds(p * size, size) for p in range(held.shape[0] // size)]
    writes = [
        pltpu.make_async_copy(held.at[part], out_ref.at[part], out_sem.at[p])
        for p, part in enumerate(parts)
    ]
    for write in writes:
        write.start()
    for write in writes:
        write.wait()


def level_chunks(own_levels):
    last = max(1, own_levels // 5)
    sizes = [own_levels - 2 * last, last, last]
    return tuple((sum(sizes[:i]), n) for i, n in enumerate(sizes) if n > 0)


def tables(width, col_total, band_total):
    length = width * col_total
    waves = np.arange(length // 4, dtype=np.int64).reshape(-1, 1, 128)
    shape = (waves.shape[0], 2, 128)
    wave_of = np.broadcast_to(waves, shape).reshape(-1)
    imaginary = np.broadcast_to(np.arange(2).reshape(1, 2, 1), shape).reshape(-1)
    angle = 2.0 * np.pi * ((np.arange(width)[:, None] * wave_of[None, :]) % length) / length
    cosine, sine = np.cos(angle), np.sin(angle)
    plain = np.where(imaginary[None, :] == 1, -sine, cosine)
    crossed = np.where(imaginary[None, :] == 1, -cosine, -sine)
    base = np.stack([plain, crossed])
    turn = 2.0 * np.pi * ((np.arange(col_total)[:, None] * wave_of[None, :]) % col_total) / col_total
    phase = np.stack([np.cos(turn), np.sin(turn)], axis=1)
    return base.astype(np.float32), phase.astype(np.float32)


def shards(fields, inverse, block_costs, row_length):
    field_total, level_total, row_total, width = fields.shape
    col_total, band_total = lax.axis_size("col"), lax.axis_size("band")
    own_levels = field_total * level_total // col_total
    vmem = pl.BlockSpec(memory_space=pltpu.VMEM)
    hbm = pl.BlockSpec(memory_space=pl.ANY)
    base, phase = tables(width, col_total, band_total)
    own_rows, piece_width = own_levels * row_total, base.shape[2] // band_total
    waves = piece_width // 2
    chunks = level_chunks(own_levels)
    table_shape = (col_total * width, base.shape[2])
    if table_shape[0] * table_shape[1] > table_limit:
        table_shape = (16, 128)
    shape = (own_levels, band_total, row_total * piece_width // 128, 128)
    spectra = pl.pallas_call(
        functools.partial(
            spectral_kernel, col_total, band_total, 1.0 / math.sqrt(width * col_total), chunks
        ),
        name="spectral",
        out_shape=pltpu.VMEM(shape, jnp.float32),
        in_specs=[hbm] * 6,
        out_specs=vmem,
        scratch_shapes=[
            pltpu.SMEM(block_costs.shape, jnp.int32),
            pltpu.SMEM(row_length.shape, jnp.int32),
            pltpu.VMEM(inverse.shape, jnp.bfloat16),
            pltpu.VMEM(phase.shape, jnp.float32),
            pltpu.VMEM(fields.shape, jnp.bfloat16),
            pltpu.VMEM((field_span, level_total * row_total, width), jnp.float32),
            pltpu.VMEM((field_span, level_total * row_total, width), jnp.float32),
            pltpu.VMEM((field_span, level_total, row_total * width), jnp.bfloat16),
            pltpu.VMEM((col_total, own_levels, row_total, width), jnp.bfloat16),
            pltpu.VMEM((col_total, own_levels, row_total, width), jnp.bfloat16),
            pltpu.VMEM((band_total, own_rows, piece_width), jnp.float32),
            pltpu.VMEM((band_total, own_rows, piece_width), jnp.bfloat16),
            pltpu.VMEM((band_total, own_rows, piece_width), jnp.bfloat16),
            pltpu.VMEM(base.shape, jnp.float32),
            pltpu.VMEM(table_shape, jnp.bfloat16),
            pltpu.SemaphoreType.DMA((field_total,)),
            pltpu.SemaphoreType.DMA((4,)),
            pltpu.SemaphoreType.DMA,
            pltpu.SemaphoreType.DMA,
            pltpu.SemaphoreType.DMA((len(chunks), col_total // min(col_total // field_total, 4))),
            pltpu.SemaphoreType.DMA((len(chunks), band_total)),
            pltpu.SemaphoreType.DMA((len(chunks), band_total)),
        ],
        compiler_params=pltpu.CompilerParams(
            collective_id=0, has_side_effects=True, vmem_limit_bytes=spectral_vmem
        ),
    )(
        *(
            pltpu.with_memory_space_constraint(value, pltpu.HBM)
            for value in (block_costs, row_length, fields, inverse, jnp.asarray(base), jnp.asarray(phase))
        )
    )
    pieces = next(p for p in (5, 4, 2, 1) if own_levels % p == 0)
    spectra = pl.pallas_call(
        functools.partial(deliver_kernel, own_levels // pieces),
        name="deliver",
        out_shape=jax.ShapeDtypeStruct(spectra.shape, spectra.dtype),
        in_specs=[vmem],
        out_specs=hbm,
        scratch_shapes=[pltpu.SemaphoreType.DMA((pieces,))],
        compiler_params=pltpu.CompilerParams(vmem_limit_bytes=deliver_vmem),
    )(spectra)
    split = spectra.reshape(own_levels, band_total * row_total, waves // 128, 2, 128)
    return split.transpose(0, 1, 3, 2, 4).reshape(own_levels, band_total * row_total, 2, waves)


def solution(mesh):
    return jax.shard_map(
        shards,
        mesh=mesh,
        in_specs=(P(None, None, "band", "col"), P(), P("col", "band"), P("band")),
        out_specs=P("col", None, None, "band"),
        check_vma=False,
    )
```
